512 devices in a mesh: row: 16 (over z, core), col: 8 (over y), layer: 4 (over x).
Axes of the slice: x: 4, y: 8, z: 8, core: 2. Of those that a mesh axis runs over, the one named last changes fastest.
Arguments:
- a_blocks: bfloat16 [4096, 128, 128], P(('row', 'col', 'layer')), may hold values from -0.5 to 0.5
- a_codes: int32 [4096], P(('row', 'col', 'layer')), may hold values from -1 to 47, as said below
- b_blocks: bfloat16 [8192, 128, 128], P(('row', 'col', 'layer')), may hold values from -6 to 6
- b_codes: int32 [8192], P(('row', 'col', 'layer')), may hold values from -1 to 23, as said below
Outputs:
- product: bfloat16 [8192, 4096], P(('row', 'layer'), 'col')
The draws below stay inside these ranges and needn't reach their ends.
Inputs may be any that keep to these rules, and one draw needn't show every extreme that they name: `a_codes`: slots that one owner receives (same o, same r and l, all q) carry distinct codes; in every group of 8 owners some owner receives 8 live slots, and every owner at least one. `b_codes`: slots that one owner receives (same o, same c and l, all q) carry distinct codes; in every group of 16 owners some owner receives 16 live slots, and every owner at least one.
All inputs are finite; a program needn't handle non-finite values.
Results may differ from the reference program's by a relative error of at most 0.001.
Values may be sent and summed in bfloat16 or wider, within the bound.
A program may use at most 64 MiB of HBM per device.

```python
import jax
import jax.numpy as jnp
from jax import lax

BS = 128
RB = 4
CB = 4
KB = 6
S_A = 8
S_B = 16
N_ROW = 16
N_COL = 8
N_LAYER = 4


def group_codes(subkey, owners, slot_count, positions):
    key_full, key_rest = jax.random.split(subkey)
    full_owner = jax.random.randint(key_full, (), 0, owners)
    owner_keys = jax.random.split(key_rest, owners)

    def one_owner(owner_key, owner_index):
        key_live, key_place, key_order = jax.random.split(owner_key, 3)
        live_count = jax.random.randint(key_live, (), 1, slot_count + 1)
        live_count = jnp.where(owner_index == full_owner, slot_count, live_count)
        placed = jax.random.permutation(key_place, positions)[:slot_count]
        order_rank = jax.random.permutation(key_order, slot_count)
        return jnp.where(order_rank < live_count, placed[order_rank], -1).astype(jnp.int32)
    return jax.vmap(one_owner)(owner_keys, jnp.arange(owners))


def draw_a_codes(key, part):
    subkeys = jax.random.split(jax.random.fold_in(key, 11), N_ROW * N_LAYER)
    positions = RB * (N_ROW // N_COL) * KB
    groups = jax.vmap(lambda subkey: group_codes(subkey, N_COL, S_A, positions))(subkeys)
    per_peer = S_A // N_COL
    owner_view = groups.reshape(N_ROW, N_LAYER, N_COL, N_COL, per_peer)
    producer_view = owner_view.transpose(0, 3, 1, 2, 4)
    return producer_view.reshape(-1).astype(jnp.int32)


def draw_b_codes(key, part):
    subkeys = jax.random.split(jax.random.fold_in(key, 23), N_COL * N_LAYER)
    positions = KB * CB
    groups = jax.vmap(lambda subkey: group_codes(subkey, N_ROW, S_B, positions))(subkeys)
    per_peer = S_B // N_ROW
    owner_view = groups.reshape(N_COL, N_LAYER, N_ROW, N_ROW, per_peer)
    producer_view = owner_view.transpose(3, 0, 1, 2, 4)
    return producer_view.reshape(-1).astype(jnp.int32)


def block_levels(own_key, dims, shards, least, top_value):
    loudness, own = 1.0, jax.random.fold_in(own_key, 6)
    for dim, shards_of in shards:
        heights = jnp.exp(jax.random.uniform(jax.random.fold_in(own, dim), (shards_of,), jnp.float32, least / len(shards), top_value / len(shards)))
        loudness = loudness * jnp.repeat(heights, dims[dim] // shards_of).reshape([-1 if axis == dim else 1 for axis in range(len(dims))])
    return loudness


def noise(stream_key, shape, scale, reach, cuts=(), kind=jnp.bfloat16):
    entries = scale * jax.random.normal(stream_key, shape, jnp.float32)
    if cuts:
        entries = entries * block_levels(stream_key, shape, cuts, -0.22, 0.18)
    return jnp.clip(entries, -reach, reach).astype(kind)


def setup_inputs(seed: int = 0) -> dict:
    splits = jax.random.split(jax.random.key(seed), 5)
    a_blocks = noise(splits[0], (N_ROW * N_COL * N_LAYER * S_A, BS, BS), BS ** -0.5, 0.5, ((0, 512),))
    a_codes = draw_a_codes(jax.random.fold_in(splits[4], 71), 0)
    b_blocks = noise(splits[2], (N_ROW * N_COL * N_LAYER * S_B, BS, BS), 1.0, 6.0, ((0, 512),))
    b_codes = draw_b_codes(jax.random.fold_in(splits[4], 71), 0)
    return {"a_blocks": a_blocks, "a_codes": a_codes, "b_blocks": b_blocks, "b_codes": b_codes}


def dense_right(block_stack, block_codes):
    is_live = block_codes >= 0
    inner_of = block_codes // CB
    column_of = block_codes % CB
    inner_hit = inner_of[:, None] == jnp.arange(KB, dtype=jnp.int32)[None, :]
    column_hit = column_of[:, None] == jnp.arange(CB, dtype=jnp.int32)[None, :]
    weight = (is_live[:, None, None] & inner_hit[:, :, None] & column_hit[:, None, :]).astype(jnp.float32)
    dense_tile = jnp.einsum("skj,sxy->kxjy", weight, block_stack.astype(jnp.float32))
    return dense_tile.astype(jnp.bfloat16).reshape(KB, BS, CB * BS)


def reference(a_blocks, a_codes, b_blocks, b_codes):
    pieces = N_ROW // N_COL
    per_peer_a = S_A // N_COL
    per_peer_b = S_B // N_ROW
    a_owned = a_blocks.reshape(N_ROW, N_COL, N_LAYER, N_COL, per_peer_a, BS, BS)
    a_owned = a_owned.transpose(0, 3, 2, 1, 4, 5, 6).reshape(N_ROW, N_COL, N_LAYER, S_A, BS, BS)
    a_tags = a_codes.reshape(N_ROW, N_COL, N_LAYER, N_COL, per_peer_a)
    a_tags = a_tags.transpose(0, 3, 2, 1, 4).reshape(N_ROW, N_COL, N_LAYER, S_A)
    b_owned = b_blocks.reshape(N_ROW, N_COL, N_LAYER, N_ROW, per_peer_b, BS, BS)
    b_owned = b_owned.transpose(3, 1, 2, 0, 4, 5, 6).reshape(N_ROW, N_COL, N_LAYER, S_B, BS, BS)
    b_tags = b_codes.reshape(N_ROW, N_COL, N_LAYER, N_ROW, per_peer_b)
    b_tags = b_tags.transpose(3, 1, 2, 0, 4).reshape(N_ROW, N_COL, N_LAYER, S_B)

    def tile_product(tile_index):
        row_index = tile_index // N_COL
        col_index = tile_index % N_COL

        def visit_piece(accumulated, visit_step):
            layer_index = visit_step // N_ROW
            piece_index = visit_step % N_ROW
            owner_a = (piece_index - row_index) % N_COL
            owner_b = (piece_index - col_index) % N_ROW
            left_stack = a_owned[row_index, owner_a, layer_index]
            left_codes = a_tags[row_index, owner_a, layer_index]
            right_tile = dense_right(b_owned[owner_b, col_index, layer_index], b_tags[owner_b, col_index, layer_index])
            is_live = left_codes >= 0
            row_of = jnp.where(is_live, left_codes // (pieces * KB), 0)
            part_of = (left_codes // KB) % pieces
            inner_of = jnp.where(is_live, left_codes % KB, 0).astype(jnp.int32)
            selected = is_live & (part_of == piece_index // N_COL)
            row_hits = (row_of[:, None] == jnp.arange(RB, dtype=jnp.int32)[None, :]) & selected[:, None]
            gathered = right_tile[inner_of]
            products = jnp.einsum("axy,ayz->axz", left_stack.astype(jnp.float32), gathered.astype(jnp.float32))
            contrib = jnp.einsum("ai,axz->ixz", row_hits.astype(jnp.float32), products)
            return accumulated + contrib.reshape(RB * BS, CB * BS), None

        start_sum = jnp.zeros((RB * BS, CB * BS), jnp.float32)
        accumulated, _ = lax.scan(visit_piece, start_sum, jnp.arange(N_LAYER * N_ROW, dtype=jnp.int32))
        return accumulated.astype(jnp.bfloat16)

    tile_sums = lax.map(tile_product, jnp.arange(N_ROW * N_COL, dtype=jnp.int32))
    tile_sums = tile_sums.reshape(N_ROW, N_COL, RB * BS, CB * BS).transpose(0, 2, 1, 3)
    return tile_sums.reshape(N_ROW * RB * BS, N_COL * CB * BS)
```

```python
import functools

import jax
import jax.numpy as jnp
from jax import lax
from jax.experimental import pallas as pl
from jax.experimental.pallas import tpu as pltpu
from jax.sharding import PartitionSpec as P

RB = 4
CB = 4
KB = 6
LANES = 128
MESH = pl.DeviceIdType.MESH


def kernel(
    rows, cols, pieces,
    a_codes, b_codes, a_in, b_in, out,
    a_all, a_tags, b_tags, table, table_s, left, right, total, passing, arrived,
    a_send, a_recv, at_send, at_recv, b_send, b_recv, p_send, p_recv,
    bt_send, bt_recv, pt_send, pt_recv, here, table_sem, x_send, x_recv,
    *b_all,
):
    chips = rows // 2
    row = lax.axis_index("row")
    col = lax.axis_index("col")
    layer = lax.axis_index("layer")
    chip, core = lax.div(row, 2), lax.rem(row, 2)
    partner = {"row": chip * 2 + 1 - core}
    empty = rows * pieces

    def row_at(step):
        return lax.rem(chip + step + chips, chips) * 2 + core

    def col_at(step):
        return lax.rem(col + step + cols, cols)

    def twin_at(step):
        return lax.rem(chip + step + chips, chips) * 2 + 1 - core

    layers = 4
    after = lax.rem(layer + 1, layers)
    before = lax.rem(layer + 3, layers)
    across = lax.rem(layer + 2, layers)

    def send(src, dst, send_sem, recv_sem, where):
        copy = pltpu.make_async_remote_copy(
            src_ref=src, dst_ref=dst, send_sem=send_sem, recv_sem=recv_sem,
            device_id=where, device_id_type=MESH,
        )
        copy.start()
        sent.append(copy)

    def wait_recv(dst, send_sem, recv_sem, where):
        pltpu.make_async_remote_copy(
            src_ref=dst, dst_ref=dst, send_sem=send_sem, recv_sem=recv_sem,
            device_id=where, device_id_type=MESH,
        ).wait_recv()

    sent = []

    lane = lax.broadcasted_iota(jnp.int32, (8, LANES), 1)
    codes = jnp.full((8, LANES), -1, jnp.int32)
    for slot in range(cols):
        codes = jnp.where(lane == slot, a_codes[slot], codes)
    a_tags[col] = codes
    slot_of = lax.broadcasted_iota(jnp.int32, (rows, LANES), 0)
    codes = jnp.full((rows, LANES), -1, jnp.int32)
    for slot in range(rows):
        codes = jnp.where(slot_of == slot, b_codes[slot], codes)
    b_tags[row] = codes
    for stack in b_all:
        stack[empty] = jnp.zeros(stack.shape[1:], stack.dtype)

    local = [pltpu.make_async_copy(a_in, a_all.at[col], here.at[cols])]
    for kind in range(cols):
        local.append(
            pltpu.make_async_copy(
                b_in.at[:, kind], b_all[kind].at[pl.ds(row * pieces, pieces)], here.at[kind]
            )
        )
    for copy in local:
        copy.start()

    barrier = pltpu.get_barrier_semaphore()
    greeted = [
        {"row": row_at(1)}, {"row": row_at(-1)}, partner,
        {"col": col_at(1)}, {"col": col_at(-1)},
        {"layer": after}, {"layer": before},
    ]
    for device in greeted:
        pl.semaphore_signal(barrier, inc=1, device_id=device, device_id_type=MESH)
    pl.semaphore_wait(barrier, len(greeted))

    half_a = cols // 2
    order = [kind for pair in zip(range(half_a), range(half_a, cols)) for kind in pair]

    def ways(kind):
        return 1 if kind < half_a else -1

    def b_place(kind, source):
        return b_all[kind].at[pl.ds(source * pieces, pieces)]

    def b_forward(kind, hop, src):
        source = row_at(-ways(kind) * hop)
        send(
            src, b_place(kind, source), b_send.at[kind, hop], b_recv.at[kind, hop],
            {"row": row_at(ways(kind))},
        )

    def b_share(kind, hop, src):
        source = row_at(-ways(kind) * hop)
        send(src, b_place(kind, source), p_send.at[kind, hop], p_recv.at[kind, hop], partner)

    def b_arrive(kind, hop):
        place = b_place(kind, row_at(-ways(kind) * hop))
        wait_recv(
            place, b_send.at[kind, hop - 1], b_recv.at[kind, hop - 1], {"row": row_at(ways(kind))}
        )
        return place

    def b_shared(kind, hop):
        wait_recv(
            b_place(kind, twin_at(-ways(kind) * hop)),
            p_send.at[kind, hop], p_recv.at[kind, hop], partner,
        )

    def a_place(way, source):
        return a_all.at[source, pl.ds(half_a * way, half_a)]

    def a_forward(way, hop, src):
        step = 1 - 2 * way
        source = col_at(-step * hop)
        send(
            src, a_place(way, source), a_send.at[way, hop], a_recv.at[way, hop],
            {"col": col_at(step)},
        )

    def a_arrive(way, hop):
        step = 1 - 2 * way
        place = a_place(way, col_at(-step * hop))
        wait_recv(place, a_send.at[way, hop - 1], a_recv.at[way, hop - 1], {"col": col_at(step)})
        return place

    def tag_reach(size, way):
        return size // 2 if way == 0 else size - 1 - size // 2

    def at_forward(way, hop):
        step = 1 - 2 * way
        place = a_tags.at[col_at(-step * hop)]
        send(place, place, at_send.at[way, hop], at_recv.at[way, hop], {"col": col_at(step)})

    def bt_forward(way, hop):
        step = 1 - 2 * way
        place = b_tags.at[row_at(-step * hop)]
        send(place, place, bt_send.at[way, hop], bt_recv.at[way, hop], {"row": row_at(step)})

    def bt_share(way, hop):
        place = b_tags.at[row_at(-(1 - 2 * way) * hop)]
        send(place, place, pt_send.at[way, hop], pt_recv.at[way, hop], partner)

    for way in range(2):
        if tag_reach(cols, way) > 0:
            at_forward(way, 0)
        if tag_reach(chips, way) > 0:
            bt_forward(way, 0)
    bt_share(0, 0)
    for index, kind in enumerate(order):
        b_forward(kind, 0, b_in.at[:, kind])
        if index < 2:
            a_forward(index, 0, a_in.at[pl.ds(half_a * index, half_a)])
    for kind in order:
        b_share(kind, 0, b_in.at[:, kind])

    def tags_step(hop):
        for way in range(2):
            step = 1 - 2 * way
            if hop <= tag_reach(cols, way):
                wait_recv(
                    a_tags.at[col_at(-step * hop)], at_send.at[way, hop - 1],
                    at_recv.at[way, hop - 1], {"col": col_at(step)},
                )
                if hop < tag_reach(cols, way):
                    at_forward(way, hop)
            if hop <= tag_reach(chips, way):
                wait_recv(
                    b_tags.at[row_at(-step * hop)], bt_send.at[way, hop - 1],
                    bt_recv.at[way, hop - 1], {"row": row_at(step)},
                )
                if hop < tag_reach(chips, way):
                    bt_forward(way, hop)
                bt_share(way, hop)

    def make_table():
        for way in range(2):
            for hop in range(0 if way == 0 else 1, tag_reach(chips, way) + 1):
                wait_recv(
                    b_tags.at[twin_at(-(1 - 2 * way) * hop)],
                    pt_send.at[way, hop], pt_recv.at[way, hop], partner,
                )
        owner = lax.broadcasted_iota(jnp.int32, (8, LANES), 0)
        tags = jnp.full((8, LANES), -1, jnp.int32)
        for source in range(cols):
            tags = jnp.where(owner == source, a_tags[source], tags)
        one = jnp.ones((8, LANES), jnp.int32)
        zero = jnp.zeros((8, LANES), jnp.int32)
        row_of = zero
        for bound in range(1, RB):
            row_of = row_of + jnp.where(tags >= bound * pieces * KB, one, zero)
        rest = tags - row_of * (pieces * KB)
        part_of = zero
        for bound in range(1, pieces):
            part_of = part_of + jnp.where(rest >= bound * KB, one, zero)
        inner_of = rest - part_of * KB
        piece = lax.rem(lane + row, cols) + cols * part_of
        live = tags >= 0
        first = jnp.where(live, (piece * KB + inner_of) * CB, -1000)
        wanted = [first + column for column in range(CB)]
        piece_b = lax.rem(slot_of + col, rows)

        def scan(source, found):
            tags_b = b_tags[source]
            position = jnp.where(tags_b >= 0, tags_b + piece_b * (KB * CB), -5000)
            found = list(found)
            for slot in range(rows):
                spot = jnp.broadcast_to(position[slot : slot + 1, :], (8, LANES))
                value = source * pieces + slot // cols
                for column in range(CB):
                    found[column] = jnp.where(wanted[column] == spot, value, found[column])
            return tuple(found)

        start = tuple(jnp.full((8, LANES), empty, jnp.int32) for _ in range(CB))
        found = lax.fori_loop(0, rows, scan, start)
        for column in range(CB):
            table[column] = found[column]
        table[CB] = jnp.where(live, row_of, -1)
        copy = pltpu.make_async_copy(table, table_s, table_sem)
        copy.start()
        copy.wait()

    def b_pass(hop):
        for kind in order:
            place = b_arrive(kind, hop)
            b_forward(kind, hop, place)
            b_share(kind, hop, place)

    def a_pass(hop):
        for way in range(2):
            place = a_arrive(way, hop)
            if hop < cols - 1:
                a_forward(way, hop, place)

    table_after = max(tag_reach(cols, 0), tag_reach(chips, 0))
    for hop in range(1, chips - 1):
        b_pass(hop)
        tags_step(hop)
        if hop < cols:
            a_pass(hop)
        if hop == table_after:
            make_table()
    for hop in range(max(chips - 1, 1), table_after + 1):
        tags_step(hop)
    if table_after >= chips - 1:
        make_table()
    for hop in range(max(chips - 1, 1), cols):
        a_pass(hop)

    def multiply(kind, is_first):
        local[1 + kind].wait()
        for hop in range(chips):
            b_shared(kind, hop)
        slot = lax.rem(kind + col + rows - row, cols)
        for source in range(cols):
            block = a_all[source, slot]
            home = table_s[CB, source, slot]
            across_k = pl.ds(source * LANES, LANES)
            for target in range(RB):
                left[pl.ds(target * LANES, LANES), across_k] = jnp.where(
                    home == target, block, jnp.zeros_like(block)
                )
            for column in range(CB):
                right[across_k, pl.ds(column * LANES, LANES)] = b_all[kind][
                    table_s[column, source, slot]
                ]
        wide = CB * LANES // 2
        for half in range(2):
            product = jnp.dot(
                left[...], right[:, pl.ds(half * wide, wide)], preferred_element_type=jnp.float32
            ).reshape(RB, LANES, wide)
            if is_first:
                total[:, half] = product
            else:
                total[:, half] = total[:, half] + product

    local[0].wait()
    pairs = [order[i : i + 2] for i in range(0, cols, 2)]
    for index, pair in enumerate(pairs + [None]):
        if pair is not None:
            for kind in pair:
                b_share(kind, chips - 1, b_arrive(kind, chips - 1))
        if index > 0:
            for kind in pairs[index - 1]:
                multiply(kind, kind == order[0])

    to_after, to_before = {"layer": after}, {"layer": before}

    def x_send_to(index, src, dst, where):
        send(src, dst, x_send.at[index], x_recv.at[index], where)

    x_send_to(0, total.at[across, 0], passing.at[0], to_after)
    x_send_to(1, total.at[across, 1], passing.at[1], to_before)
    x_send_to(2, total.at[after, 1], arrived.at[0, 1], to_after)
    x_send_to(3, total.at[before, 0], arrived.at[1, 0], to_before)
    wait_recv(passing.at[0], x_send.at[0], x_recv.at[0], to_after)
    total[after, 0] = total[after, 0] + passing[0]
    x_send_to(4, total.at[after, 0], arrived.at[0, 0], to_after)
    wait_recv(passing.at[1], x_send.at[1], x_recv.at[1], to_before)
    total[before, 1] = total[before, 1] + passing[1]
    x_send_to(5, total.at[before, 1], arrived.at[1, 1], to_before)
    wait_recv(arrived.at[0, 1], x_send.at[2], x_recv.at[2], to_after)
    wait_recv(arrived.at[1, 0], x_send.at[3], x_recv.at[3], to_before)
    wait_recv(arrived.at[0, 0], x_send.at[4], x_recv.at[4], to_after)
    wait_recv(arrived.at[1, 1], x_send.at[5], x_recv.at[5], to_before)
    wide = CB * LANES // 2
    for half in range(2):
        out[:, pl.ds(half * wide, wide)] = (
            total[layer, half] + arrived[0, half] + arrived[1, half]
        ).astype(out.dtype)
    for copy in sent:
        copy.wait_send()


def shards(a_blocks, a_codes, b_blocks, b_codes):
    rows = lax.axis_size("row")
    cols = lax.axis_size("col")
    pieces = rows // cols
    chips = rows // 2
    size = a_blocks.shape[1]
    b_blocks = b_blocks.reshape(pieces, cols, size, size)
    anywhere = pl.BlockSpec(memory_space=pl.ANY)
    scalars = pl.BlockSpec(memory_space=pltpu.SMEM)
    dma = pltpu.SemaphoreType.DMA
    wide = CB * size // 2
    scratch = [
        pltpu.VMEM((cols, cols, size, size), jnp.bfloat16),
        pltpu.VMEM((cols, 8, LANES), jnp.int32),
        pltpu.VMEM((rows, rows, LANES), jnp.int32),
        pltpu.VMEM((CB + 1, 8, LANES), jnp.int32),
        pltpu.SMEM((CB + 1, 8, LANES), jnp.int32),
        pltpu.VMEM((RB * size, cols * size), jnp.bfloat16),
        pltpu.VMEM((cols * size, CB * size), jnp.bfloat16),
        pltpu.VMEM((RB, 2, size, wide), jnp.float32),
        pltpu.VMEM((2, size, wide), jnp.float32),
        pltpu.VMEM((2, 2, size, wide), jnp.float32),
        dma((2, cols)), dma((2, cols)), dma((2, cols)), dma((2, cols)),
        dma((cols, chips)), dma((cols, chips)), dma((cols, chips)), dma((cols, chips)),
        dma((2, chips)), dma((2, chips)), dma((2, chips)), dma((2, chips)),
        dma((cols + 1,)), dma(()), dma((6,)), dma((6,)),
    ] + [pltpu.VMEM((rows * pieces + 1, size, size), jnp.bfloat16)] * cols
    return pl.pallas_call(
        functools.partial(kernel, rows, cols, pieces),
        out_shape=jax.ShapeDtypeStruct((size, CB * size), jnp.bfloat16),
        in_specs=[scalars, scalars, anywhere, anywhere],
        out_specs=pl.BlockSpec(memory_space=pltpu.VMEM),
        scratch_shapes=scratch,
        compiler_params=pltpu.CompilerParams(
            collective_id=0, has_side_effects=True, vmem_limit_bytes=32 * 1024 * 1024
        ),
        name="gather_multiply_scatter",
    )(a_codes, b_codes, a_blocks, b_blocks)


def solution(mesh):
    placed = (
        P(("row", "col", "layer"), None, None),
        P(("row", "col", "layer")),
        P(("row", "col", "layer"), None, None),
        P(("row", "col", "layer")),
    )
    return jax.shard_map(
        shards, mesh=mesh, in_specs=placed, out_specs=P(("row", "layer"), "col"), check_vma=False
    )
```

```python
import functools

import jax
import jax.numpy as jnp
from jax import lax
from jax.experimental import pallas as pl
from jax.experimental.pallas import tpu as pltpu
from jax.sharding import PartitionSpec as P

RB = 4
CB = 4
KB = 6
LANES = 128
MESH = pl.DeviceIdType.MESH


def kernel(
    rows, cols, pieces,
    a_codes, b_codes, a_in, b_in, out,
    a_all, a_tags, b_tags, table, table_s, left, right, total, passing, arrived,
    a_send, a_recv, at_send, at_recv, b_send, b_recv, p_send, p_recv,
    bt_send, bt_recv, pt_send, pt_recv, here, table_sem, x_send, x_recv,
    *b_all,
):
    chips = rows // 2
    row = lax.axis_index("row")
    col = lax.axis_index("col")
    layer = lax.axis_index("layer")
    chip, core = lax.div(row, 2), lax.rem(row, 2)
    partner = {"row": chip * 2 + 1 - core}
    empty = rows * pieces

    def row_at(step):
        return lax.rem(chip + step + chips, chips) * 2 + core

    def col_at(step):
        return lax.rem(col + step + cols, cols)

    def twin_at(step):
        return lax.rem(chip + step + chips, chips) * 2 + 1 - core

    layers = 4
    after = lax.rem(layer + 1, layers)
    before = lax.rem(layer + 3, layers)
    across = lax.rem(layer + 2, layers)

    def send(src, dst, send_sem, recv_sem, where):
        copy = pltpu.make_async_remote_copy(
            src_ref=src, dst_ref=dst, send_sem=send_sem, recv_sem=recv_sem,
            device_id=where, device_id_type=MESH,
        )
        copy.start()
        sent.append(copy)

    def wait_recv(dst, send_sem, recv_sem, where):
        pltpu.make_async_remote_copy(
            src_ref=dst, dst_ref=dst, send_sem=send_sem, recv_sem=recv_sem,
            device_id=where, device_id_type=MESH,
        ).wait_recv()

    sent = []

    lane = lax.broadcasted_iota(jnp.int32, (8, LANES), 1)
    codes = jnp.full((8, LANES), -1, jnp.int32)
    for slot in range(cols):
        codes = jnp.where(lane == slot, a_codes[slot], codes)
    a_tags[col] = codes
    slot_of = lax.broadcasted_iota(jnp.int32, (rows, LANES), 0)
    codes = jnp.full((rows, LANES), -1, jnp.int32)
    for slot in range(rows):
        codes = jnp.where(slot_of == slot, b_codes[slot], codes)
    b_tags[row] = codes
    for stack in b_all:
        stack[empty] = jnp.zeros(stack.shape[1:], stack.dtype)

    local = [pltpu.make_async_copy(a_in, a_all.at[col], here.at[cols])]
    for kind in range(cols):
        local.append(
            pltpu.make_async_copy(
                b_in.at[:, kind], b_all[kind].at[pl.ds(row * pieces, pieces)], here.at[kind]
            )
        )
    for copy in local:
        copy.start()

    barrier = pltpu.get_barrier_semaphore()
    greeted = [
        {"row": row_at(1)}, {"row": row_at(-1)}, partner,
        {"col": col_at(1)}, {"col": col_at(-1)},
        {"layer": after}, {"layer": before},
    ]
    for device in greeted:
        pl.semaphore_signal(barrier, inc=1, device_id=device, device_id_type=MESH)
    pl.semaphore_wait(barrier, len(greeted))

    half_a = cols // 2
    order = [kind for pair in zip(range(half_a), range(half_a, cols)) for kind in pair]

    def ways(kind):
        return 1 if kind < half_a else -1

    def b_place(kind, source):
        return b_all[kind].at[pl.ds(source * pieces, pieces)]

    def b_forward(kind, hop, src):
        source = row_at(-ways(kind) * hop)
        send(
            src, b_place(kind, source), b_send.at[kind, hop], b_recv.at[kind, hop],
            {"row": row_at(ways(kind))},
        )

    def b_share(kind, hop, src):
        source = row_at(-ways(kind) * hop)
        send(src, b_place(kind, source), p_send.at[kind, hop], p_recv.at[kind, hop], partner)

    def b_arrive(kind, hop):
        place = b_place(kind, row_at(-ways(kind) * hop))
        wait_recv(
            place, b_send.at[kind, hop - 1], b_recv.at[kind, hop - 1], {"row": row_at(ways(kind))}
        )
        return place

    def b_shared(kind, hop):
        wait_recv(
            b_place(kind, twin_at(-ways(kind) * hop)),
            p_send.at[kind, hop], p_recv.at[kind, hop], partner,
        )

    def a_place(way, source):
        return a_all.at[source, pl.ds(half_a * way, half_a)]

    def a_forward(way, hop, src):
        step = 1 - 2 * way
        source = col_at(-step * hop)
        send(
            src, a_place(way, source), a_send.at[way, hop], a_recv.at[way, hop],
            {"col": col_at(step)},
        )

    def a_arrive(way, hop):
        step = 1 - 2 * way
        place = a_place(way, col_at(-step * hop))
        wait_recv(place, a_send.at[way, hop - 1], a_recv.at[way, hop - 1], {"col": col_at(step)})
        return place

    def tag_reach(size, way):
        return size // 2 if way == 0 else size - 1 - size // 2

    def at_forward(way, hop):
        step = 1 - 2 * way
        place = a_tags.at[col_at(-step * hop)]
        send(place, place, at_send.at[way, hop], at_recv.at[way, hop], {"col": col_at(step)})

    def bt_forward(way, hop):
        step = 1 - 2 * way
        place = b_tags.at[row_at(-step * hop)]
        send(place, place, bt_send.at[way, hop], bt_recv.at[way, hop], {"row": row_at(step)})

    def bt_share(way, hop):
        place = b_tags.at[row_at(-(1 - 2 * way) * hop)]
        send(place, place, pt_send.at[way, hop], pt_recv.at[way, hop], partner)

    for way in range(2):
        if tag_reach(cols, way) > 0:
            at_forward(way, 0)
        if tag_reach(chips, way) > 0:
            bt_forward(way, 0)
    bt_share(0, 0)
    for index, kind in enumerate(order):
        b_forward(kind, 0, b_in.at[:, kind])
        if index < 2:
            a_forward(index, 0, a_in.at[pl.ds(half_a * index, half_a)])
    for kind in order:
        b_share(kind, 0, b_in.at[:, kind])

    def tags_step(hop):
        for way in range(2):
            step = 1 - 2 * way
            if hop <= tag_reach(cols, way):
                wait_recv(
                    a_tags.at[col_at(-step * hop)], at_send.at[way, hop - 1],
                    at_recv.at[way, hop - 1], {"col": col_at(step)},
                )
                if hop < tag_reach(cols, way):
                    at_forward(way, hop)
            if hop <= tag_reach(chips, way):
                wait_recv(
                    b_tags.at[row_at(-step * hop)], bt_send.at[way, hop - 1],
                    bt_recv.at[way, hop - 1], {"row": row_at(step)},
                )
                if hop < tag_reach(chips, way):
                    bt_forward(way, hop)
                bt_share(way, hop)

    def make_table():
        for way in range(2):
            for hop in range(0 if way == 0 else 1, tag_reach(chips, way) + 1):
                wait_recv(
                    b_tags.at[twin_at(-(1 - 2 * way) * hop)],
                    pt_send.at[way, hop], pt_recv.at[way, hop], partner,
                )
        owner = lax.broadcasted_iota(jnp.int32, (8, LANES), 0)
        tags = jnp.full((8, LANES), -1, jnp.int32)
        for source in range(cols):
            tags = jnp.where(owner == source, a_tags[source], tags)
        one = jnp.ones((8, LANES), jnp.int32)
        zero = jnp.zeros((8, LANES), jnp.int32)
        row_of = zero
        for bound in range(1, RB):
            row_of = row_of + jnp.where(tags >= bound * pieces * KB, one, zero)
        rest = tags - row_of * (pieces * KB)
        part_of = zero
        for bound in range(1, pieces):
            part_of = part_of + jnp.where(rest >= bound * KB, one, zero)
        inner_of = rest - part_of * KB
        piece = lax.rem(lane + row, cols) + cols * part_of
        live = tags >= 0
        first = jnp.where(live, (piece * KB + inner_of) * CB, -1000)
        wanted = [first + column for column in range(CB)]
        piece_b = lax.rem(slot_of + col, rows)

        def scan(source, found):
            tags_b = b_tags[source]
            position = jnp.where(tags_b >= 0, tags_b + piece_b * (KB * CB), -5000)
            found = list(found)
            for slot in range(rows):
                spot = jnp.broadcast_to(position[slot : slot + 1, :], (8, LANES))
                value = source * pieces + slot // cols
                for column in range(CB):
                    found[column] = jnp.where(wanted[column] == spot, value, found[column])
            return tuple(found)

        start = tuple(jnp.full((8, LANES), empty, jnp.int32) for _ in range(CB))
        found = lax.fori_loop(0, rows, scan, start)
        for column in range(CB):
            table[column] = found[column]
        table[CB] = jnp.where(live, row_of, -1)
        copy = pltpu.make_async_copy(table, table_s, table_sem)
        copy.start()
        copy.wait()

    def a_pass(hop):
        for way in range(2):
            place = a_arrive(way, hop)
            if hop < cols - 1:
                a_forward(way, hop, place)

    homes = [across, after, before, layer]

    def slot_for(kind):
        return lax.rem(kind + col + rows - row, cols)

    def place_left(kind):
        slot = slot_for(kind)
        for source in range(cols):
            block = a_all[source, slot]
            home = table_s[CB, source, slot]
            for target in range(RB):
                left[kind, pl.ds(target * LANES, LANES), pl.ds(source * LANES, LANES)] = (
                    jnp.where(home == homes[target], block, jnp.zeros_like(block))
                )

    def place_right(kind, index):
        local[1 + kind].wait()
        for hop in range(chips):
            b_shared(kind, hop)
        slot = slot_for(kind)
        for source in range(cols):
            for column in range(CB):
                right[index, pl.ds(source * LANES, LANES), pl.ds(column * LANES, LANES)] = (
                    b_all[kind][table_s[column, source, slot]]
                )

    wide = CB * LANES // 2

    def multiply(kinds, first_row, row_count, is_first):
        for half in range(2):
            product = None
            for index, kind in enumerate(kinds):
                term = jnp.dot(
                    left[kind, pl.ds(first_row * LANES, row_count * LANES), :],
                    right[index, :, pl.ds(half * wide, wide)],
                    preferred_element_type=jnp.float32,
                )
                product = term if product is None else product + term
            product = product.reshape(row_count, LANES, wide)
            part = pl.ds(first_row, row_count)
            total[part, half] = product if is_first else total[part, half] + product

    table_after = max(tag_reach(cols, 0), tag_reach(chips, 0))
    progress = {"a": 1, "table": False, "left": 0}

    def a_until(event):
        while progress["a"] < cols and event >= 7 * progress["a"] - 5:
            a_pass(progress["a"])
            progress["a"] += 1
            if progress["a"] == cols:
                local[0].wait()

    def one_left():
        if progress["a"] == cols and progress["table"] and progress["left"] < cols:
            place_left(order[progress["left"]])
            progress["left"] += 1

    for hop in range(1, chips - 1):
        for index, kind in enumerate(order):
            place = b_arrive(kind, hop)
            b_forward(kind, hop, place)
            b_share(kind, hop, place)
            a_until((hop - 1) * cols + index)
            one_left()
        tags_step(hop)
        if hop == table_after:
            make_table()
            progress["table"] = True
    for hop in range(max(chips - 1, 1), table_after + 1):
        tags_step(hop)
    if not progress["table"]:
        make_table()
        progress["table"] = True
    a_until(7 * cols)

    pairs = [order[i : i + 2] for i in range(0, cols, 2)]
    early = pairs[: max(len(pairs) - 2, 0)]
    late = [kind for pair in pairs[len(early) :] for kind in pair]

    def finish(pair):
        for kind in pair:
            b_share(kind, chips - 1, b_arrive(kind, chips - 1))
            one_left()

    finish(pairs[0])
    for index, pair in enumerate(pairs):
        if index + 1 < len(pairs):
            finish(pairs[index + 1])
        if pair in early:
            for part, kind in enumerate(pair):
                place_right(kind, part)
            multiply(pair, 0, RB, index == 0)
    for index, kind in enumerate(late):
        place_right(kind, index)

    to_after, to_before = {"layer": after}, {"layer": before}

    def x_send_to(index, src, dst, where):
        send(src, dst, x_send.at[index], x_recv.at[index], where)

    multiply(late, 0, 1, not early)
    x_send_to(0, total.at[0, 0], passing.at[0], to_after)
    x_send_to(1, total.at[0, 1], passing.at[1], to_before)
    multiply(late, 1, 2, not early)
    x_send_to(2, total.at[1, 1], arrived.at[0, 1], to_after)
    x_send_to(3, total.at[2, 0], arrived.at[1, 0], to_before)
    multiply(late, 3, 1, not early)
    wait_recv(passing.at[0], x_send.at[0], x_recv.at[0], to_after)
    total[1, 0] = total[1, 0] + passing[0]
    x_send_to(4, total.at[1, 0], arrived.at[0, 0], to_after)
    wait_recv(passing.at[1], x_send.at[1], x_recv.at[1], to_before)
    total[2, 1] = total[2, 1] + passing[1]
    x_send_to(5, total.at[2, 1], arrived.at[1, 1], to_before)
    wait_recv(arrived.at[0, 1], x_send.at[2], x_recv.at[2], to_after)
    wait_recv(arrived.at[1, 0], x_send.at[3], x_recv.at[3], to_before)
    wait_recv(arrived.at[0, 0], x_send.at[4], x_recv.at[4], to_after)
    wait_recv(arrived.at[1, 1], x_send.at[5], x_recv.at[5], to_before)
    for half in range(2):
        out[:, pl.ds(half * wide, wide)] = (
            total[3, half] + arrived[0, half] + arrived[1, half]
        ).astype(out.dtype)
    for copy in sent:
        copy.wait_send()


def shards(a_blocks, a_codes, b_blocks, b_codes):
    rows = lax.axis_size("row")
    cols = lax.axis_size("col")
    pieces = rows // cols
    chips = rows // 2
    size = a_blocks.shape[1]
    b_blocks = b_blocks.reshape(pieces, cols, size, size)
    anywhere = pl.BlockSpec(memory_space=pl.ANY)
    scalars = pl.BlockSpec(memory_space=pltpu.SMEM)
    dma = pltpu.SemaphoreType.DMA
    wide = CB * size // 2
    scratch = [
        pltpu.VMEM((cols, cols, size, size), jnp.bfloat16),
        pltpu.VMEM((cols, 8, LANES), jnp.int32),
        pltpu.VMEM((rows, rows, LANES), jnp.int32),
        pltpu.VMEM((CB + 1, 8, LANES), jnp.int32),
        pltpu.SMEM((CB + 1, 8, LANES), jnp.int32),
        pltpu.VMEM((cols, RB * size, cols * size), jnp.bfloat16),
        pltpu.VMEM((4, cols * size, CB * size), jnp.bfloat16),
        pltpu.VMEM((RB, 2, size, wide), jnp.float32),
        pltpu.VMEM((2, size, wide), jnp.float32),
        pltpu.VMEM((2, 2, size, wide), jnp.float32),
        dma((2, cols)), dma((2, cols)), dma((2, cols)), dma((2, cols)),
        dma((cols, chips)), dma((cols, chips)), dma((cols, chips)), dma((cols, chips)),
        dma((2, chips)), dma((2, chips)), dma((2, chips)), dma((2, chips)),
        dma((cols + 1,)), dma(()), dma((6,)), dma((6,)),
    ] + [pltpu.VMEM((rows * pieces + 1, size, size), jnp.bfloat16)] * cols
    return pl.pallas_call(
        functools.partial(kernel, rows, cols, pieces),
        out_shape=jax.ShapeDtypeStruct((size, CB * size), jnp.bfloat16),
        in_specs=[scalars, scalars, anywhere, anywhere],
        out_specs=pl.BlockSpec(memory_space=pltpu.VMEM),
        scratch_shapes=scratch,
        compiler_params=pltpu.CompilerParams(
            collective_id=0, has_side_effects=True, vmem_limit_bytes=62 * 1024 * 1024
        ),
        name="gather_multiply_scatter",
    )(a_codes, b_codes, a_blocks, b_blocks)


def solution(mesh):
    placed = (
        P(("row", "col", "layer"), None, None),
        P(("row", "col", "layer")),
        P(("row", "col", "layer"), None, None),
        P(("row", "col", "layer")),
    )
    return jax.shard_map(
        shards, mesh=mesh, in_specs=placed, out_specs=P(("row", "layer"), "col"), check_vma=False
    )
```

```python
import functools

import jax
import jax.numpy as jnp
from jax import lax
from jax.experimental import pallas as pl
from jax.experimental.pallas import tpu as pltpu
from jax.sharding import PartitionSpec as P

RB = 4
CB = 4
KB = 6
LANES = 128
MESH = pl.DeviceIdType.MESH


def kernel(
    rows, cols, pieces,
    a_codes, b_codes, a_in, b_in, out,
    a_all, a_tags, b_tags, table, table_s, left, right, total, passing, arrived,
    a_send, a_recv, at_send, at_recv, b_send, b_recv, p_send, p_recv,
    bt_send, bt_recv, pt_send, pt_recv, here, table_sem, x_send, x_recv,
    *b_all,
):
    chips = rows // 2
    row = lax.axis_index("row")
    col = lax.axis_index("col")
    layer = lax.axis_index("layer")
    chip, core = lax.div(row, 2), lax.rem(row, 2)
    partner = {"row": chip * 2 + 1 - core}
    empty = rows * pieces

    def row_at(step):
        return lax.rem(chip + step + chips, chips) * 2 + core

    def col_at(step):
        return lax.rem(col + step + cols, cols)

    def twin_at(step):
        return lax.rem(chip + step + chips, chips) * 2 + 1 - core

    layers = 4
    after = lax.rem(layer + 1, layers)
    before = lax.rem(layer + 3, layers)
    across = lax.rem(layer + 2, layers)

    def send(src, dst, send_sem, recv_sem, where):
        copy = pltpu.make_async_remote_copy(
            src_ref=src, dst_ref=dst, send_sem=send_sem, recv_sem=recv_sem,
            device_id=where, device_id_type=MESH,
        )
        copy.start()
        sent.append(copy)

    def wait_recv(dst, send_sem, recv_sem, where):
        pltpu.make_async_remote_copy(
            src_ref=dst, dst_ref=dst, send_sem=send_sem, recv_sem=recv_sem,
            device_id=where, device_id_type=MESH,
        ).wait_recv()

    sent = []

    lane = lax.broadcasted_iota(jnp.int32, (8, LANES), 1)
    codes = jnp.full((8, LANES), -1, jnp.int32)
    for slot in range(cols):
        codes = jnp.where(lane == slot, a_codes[slot], codes)
    a_tags[col] = codes
    slot_of = lax.broadcasted_iota(jnp.int32, (rows, LANES), 0)
    codes = jnp.full((rows, LANES), -1, jnp.int32)
    for slot in range(rows):
        codes = jnp.where(slot_of == slot, b_codes[slot], codes)
    b_tags[row] = codes
    for stack in b_all:
        stack[empty] = jnp.zeros(stack.shape[1:], stack.dtype)

    local = [pltpu.make_async_copy(a_in, a_all.at[col], here.at[cols])]
    for kind in range(cols):
        local.append(
            pltpu.make_async_copy(
                b_in.at[:, kind], b_all[kind].at[pl.ds(row * pieces, pieces)], here.at[kind]
            )
        )
    for copy in local:
        copy.start()

    barrier = pltpu.get_barrier_semaphore()
    greeted = [
        {"row": row_at(1)}, {"row": row_at(-1)}, partner,
        {"col": col_at(1)}, {"col": col_at(-1)},
        {"layer": after}, {"layer": before},
    ]
    for device in greeted:
        pl.semaphore_signal(barrier, inc=1, device_id=device, device_id_type=MESH)
    pl.semaphore_wait(barrier, len(greeted))

    half_a = cols // 2
    order = [kind for pair in zip(range(half_a), range(half_a, cols)) for kind in pair]

    def ways(kind):
        return 1 if kind < half_a else -1

    def b_place(kind, source):
        return b_all[kind].at[pl.ds(source * pieces, pieces)]

    def b_forward(kind, hop, src):
        source = row_at(-ways(kind) * hop)
        send(
            src, b_place(kind, source), b_send.at[kind, hop], b_recv.at[kind, hop],
            {"row": row_at(ways(kind))},
        )

    def b_share(kind, hop, src):
        source = row_at(-ways(kind) * hop)
        send(src, b_place(kind, source), p_send.at[kind, hop], p_recv.at[kind, hop], partner)

    def b_arrive(kind, hop):
        place = b_place(kind, row_at(-ways(kind) * hop))
        wait_recv(
            place, b_send.at[kind, hop - 1], b_recv.at[kind, hop - 1], {"row": row_at(ways(kind))}
        )
        return place

    def b_shared(kind, hop):
        wait_recv(
            b_place(kind, twin_at(-ways(kind) * hop)),
            p_send.at[kind, hop], p_recv.at[kind, hop], partner,
        )

    def a_place(way, source):
        return a_all.at[source, pl.ds(half_a * way, half_a)]

    def a_forward(way, hop, src):
        step = 1 - 2 * way
        source = col_at(-step * hop)
        send(
            src, a_place(way, source), a_send.at[way, hop], a_recv.at[way, hop],
            {"col": col_at(step)},
        )

    def a_arrive(way, hop):
        step = 1 - 2 * way
        place = a_place(way, col_at(-step * hop))
        wait_recv(place, a_send.at[way, hop - 1], a_recv.at[way, hop - 1], {"col": col_at(step)})
        return place

    def tag_reach(size, way):
        return size // 2 if way == 0 else size - 1 - size // 2

    def at_forward(way, hop):
        step = 1 - 2 * way
        place = a_tags.at[col_at(-step * hop)]
        send(place, place, at_send.at[way, hop], at_recv.at[way, hop], {"col": col_at(step)})

    def bt_forward(way, hop):
        step = 1 - 2 * way
        place = b_tags.at[row_at(-step * hop)]
        send(place, place, bt_send.at[way, hop], bt_recv.at[way, hop], {"row": row_at(step)})

    def bt_share(way, hop):
        place = b_tags.at[row_at(-(1 - 2 * way) * hop)]
        send(place, place, pt_send.at[way, hop], pt_recv.at[way, hop], partner)

    for index, kind in enumerate(order):
        b_forward(kind, 0, b_in.at[:, kind])
        if index == 1:
            for way in range(2):
                if tag_reach(cols, way) > 0:
                    at_forward(way, 0)
                if tag_reach(chips, way) > 0:
                    bt_forward(way, 0)
            bt_share(0, 0)
            for way in range(2):
                a_forward(way, 0, a_in.at[pl.ds(half_a * way, half_a)])
    for kind in order:
        b_share(kind, 0, b_in.at[:, kind])

    def tags_step(hop):
        for way in range(2):
            step = 1 - 2 * way
            if hop <= tag_reach(cols, way):
                wait_recv(
                    a_tags.at[col_at(-step * hop)], at_send.at[way, hop - 1],
                    at_recv.at[way, hop - 1], {"col": col_at(step)},
                )
                if hop < tag_reach(cols, way):
                    at_forward(way, hop)
            if hop <= tag_reach(chips, way):
                wait_recv(
                    b_tags.at[row_at(-step * hop)], bt_send.at[way, hop - 1],
                    bt_recv.at[way, hop - 1], {"row": row_at(step)},
                )
                if hop < tag_reach(chips, way):
                    bt_forward(way, hop)
                bt_share(way, hop)

    def make_table():
        for way in range(2):
            for hop in range(0 if way == 0 else 1, tag_reach(chips, way) + 1):
                wait_recv(
                    b_tags.at[twin_at(-(1 - 2 * way) * hop)],
                    pt_send.at[way, hop], pt_recv.at[way, hop], partner,
                )
        owner = lax.broadcasted_iota(jnp.int32, (8, LANES), 0)
        tags = jnp.full((8, LANES), -1, jnp.int32)
        for source in range(cols):
            tags = jnp.where(owner == source, a_tags[source], tags)
        one = jnp.ones((8, LANES), jnp.int32)
        zero = jnp.zeros((8, LANES), jnp.int32)
        row_of = zero
        for bound in range(1, RB):
            row_of = row_of + jnp.where(tags >= bound * pieces * KB, one, zero)
        rest = tags - row_of * (pieces * KB)
        part_of = zero
        for bound in range(1, pieces):
            part_of = part_of + jnp.where(rest >= bound * KB, one, zero)
        inner_of = rest - part_of * KB
        piece = lax.rem(lane + row, cols) + cols * part_of
        live = tags >= 0
        first = jnp.where(live, (piece * KB + inner_of) * CB, -1000)
        wanted = [first + column for column in range(CB)]
        piece_b = lax.rem(slot_of + col, rows)

        def scan(source, found):
            tags_b = b_tags[source]
            position = jnp.where(tags_b >= 0, tags_b + piece_b * (KB * CB), -5000)
            found = list(found)
            for slot in range(rows):
                spot = jnp.broadcast_to(position[slot : slot + 1, :], (8, LANES))
                value = source * pieces + slot // cols
                for column in range(CB):
                    found[column] = jnp.where(wanted[column] == spot, value, found[column])
            return tuple(found)

        start = tuple(jnp.full((8, LANES), empty, jnp.int32) for _ in range(CB))
        found = lax.fori_loop(0, rows, scan, start)
        for column in range(CB):
            table[column] = found[column]
        table[CB] = jnp.where(live, row_of, -1)
        copy = pltpu.make_async_copy(table, table_s, table_sem)
        copy.start()
        copy.wait()

    def a_pass(hop):
        for way in range(2):
            place = a_arrive(way, hop)
            if hop < cols - 1:
                a_forward(way, hop, place)

    homes = [across, after, before, layer]

    def slot_for(kind):
        return lax.rem(kind + col + rows - row, cols)

    def place_left(kind):
        slot = slot_for(kind)
        for source in range(cols):
            block = a_all[source, slot]
            home = table_s[CB, source, slot]
            for target in range(RB):
                left[kind, pl.ds(target * LANES, LANES), pl.ds(source * LANES, LANES)] = (
                    jnp.where(home == homes[target], block, jnp.zeros_like(block))
                )

    def place_right(kind, index):
        local[1 + kind].wait()
        for hop in range(chips):
            b_shared(kind, hop)
        slot = slot_for(kind)
        for source in range(cols):
            for column in range(CB):
                right[index, pl.ds(source * LANES, LANES), pl.ds(column * LANES, LANES)] = (
                    b_all[kind][table_s[column, source, slot]]
                )

    wide = CB * LANES // 2

    def multiply(kinds, first_row, row_count, is_first):
        for half in range(2):
            product = None
            for index, kind in enumerate(kinds):
                term = jnp.dot(
                    left[kind, pl.ds(first_row * LANES, row_count * LANES), :],
                    right[index, :, pl.ds(half * wide, wide)],
                    preferred_element_type=jnp.float32,
                )
                product = term if product is None else product + term
            product = product.reshape(row_count, LANES, wide)
            part = pl.ds(first_row, row_count)
            total[part, half] = product if is_first else total[part, half] + product

    table_after = max(tag_reach(cols, 0), tag_reach(chips, 0))
    progress = {"a": 1, "table": False, "left": 0}

    def a_until(event):
        while progress["a"] < cols and event >= 7 * progress["a"] - 5:
            a_pass(progress["a"])
            progress["a"] += 1
            if progress["a"] == cols:
                local[0].wait()

    def one_left():
        if progress["a"] == cols and progress["table"] and progress["left"] < cols:
            place_left(order[progress["left"]])
            progress["left"] += 1

    for hop in range(1, chips - 1):
        for index, kind in enumerate(order):
            place = b_arrive(kind, hop)
            b_forward(kind, hop, place)
            b_share(kind, hop, place)
            a_until((hop - 1) * cols + index)
            one_left()
        tags_step(hop)
        if hop == table_after:
            make_table()
            progress["table"] = True
    for hop in range(max(chips - 1, 1), table_after + 1):
        tags_step(hop)
    if not progress["table"]:
        make_table()
        progress["table"] = True
    a_until(7 * cols)

    pairs = [order[i : i + 2] for i in range(0, cols, 2)]
    early = pairs[: max(len(pairs) - 1, 0)]
    late = [kind for pair in pairs[len(early) :] for kind in pair]

    def finish(pair):
        for kind in pair:
            b_share(kind, chips - 1, b_arrive(kind, chips - 1))
            one_left()

    finish(pairs[0])
    for index, pair in enumerate(pairs):
        if index + 1 < len(pairs):
            finish(pairs[index + 1])
        if pair in early:
            for part, kind in enumerate(pair):
                place_right(kind, part)
            multiply(pair, 0, RB, index == 0)
    for index, kind in enumerate(late):
        place_right(kind, index)

    to_after, to_before = {"layer": after}, {"layer": before}

    def x_send_to(index, src, dst, where):
        send(src, dst, x_send.at[index], x_recv.at[index], where)

    multiply(late, 0, 1, not early)
    x_send_to(0, total.at[0, 0], passing.at[0], to_after)
    x_send_to(1, total.at[0, 1], passing.at[1], to_before)
    multiply(late, 1, 2, not early)
    x_send_to(2, total.at[1, 1], arrived.at[0, 1], to_after)
    x_send_to(3, total.at[2, 0], arrived.at[1, 0], to_before)
    multiply(late, 3, 1, not early)
    wait_recv(passing.at[0], x_send.at[0], x_recv.at[0], to_after)
    total[1, 0] = total[1, 0] + passing[0]
    x_send_to(4, total.at[1, 0], arrived.at[0, 0], to_after)
    wait_recv(passing.at[1], x_send.at[1], x_recv.at[1], to_before)
    total[2, 1] = total[2, 1] + passing[1]
    x_send_to(5, total.at[2, 1], arrived.at[1, 1], to_before)
    for copy in sent:
        copy.wait_send()
    wait_recv(arrived.at[0, 1], x_send.at[2], x_recv.at[2], to_after)
    wait_recv(arrived.at[1, 0], x_send.at[3], x_recv.at[3], to_before)
    wait_recv(arrived.at[0, 0], x_send.at[4], x_recv.at[4], to_after)
    wait_recv(arrived.at[1, 1], x_send.at[5], x_recv.at[5], to_before)
    for half in range(2):
        out[:, pl.ds(half * wide, wide)] = (
            total[3, half] + arrived[0, half] + arrived[1, half]
        ).astype(out.dtype)


def shards(a_blocks, a_codes, b_blocks, b_codes):
    rows = lax.axis_size("row")
    cols = lax.axis_size("col")
    pieces = rows // cols
    chips = rows // 2
    size = a_blocks.shape[1]
    b_blocks = b_blocks.reshape(pieces, cols, size, size)
    anywhere = pl.BlockSpec(memory_space=pl.ANY)
    scalars = pl.BlockSpec(memory_space=pltpu.SMEM)
    dma = pltpu.SemaphoreType.DMA
    wide = CB * size // 2
    scratch = [
        pltpu.VMEM((cols, cols, size, size), jnp.bfloat16),
        pltpu.VMEM((cols, 8, LANES), jnp.int32),
        pltpu.VMEM((rows, rows, LANES), jnp.int32),
        pltpu.VMEM((CB + 1, 8, LANES), jnp.int32),
        pltpu.SMEM((CB + 1, 8, LANES), jnp.int32),
        pltpu.VMEM((cols, RB * size, cols * size), jnp.bfloat16),
        pltpu.VMEM((4, cols * size, CB * size), jnp.bfloat16),
        pltpu.VMEM((RB, 2, size, wide), jnp.float32),
        pltpu.VMEM((2, size, wide), jnp.float32),
        pltpu.VMEM((2, 2, size, wide), jnp.float32),
        dma((2, cols)), dma((2, cols)), dma((2, cols)), dma((2, cols)),
        dma((cols, chips)), dma((cols, chips)), dma((cols, chips)), dma((cols, chips)),
        dma((2, chips)), dma((2, chips)), dma((2, chips)), dma((2, chips)),
        dma((cols + 1,)), dma(()), dma((6,)), dma((6,)),
    ] + [pltpu.VMEM((rows * pieces + 1, size, size), jnp.bfloat16)] * cols
    return pl.pallas_call(
        functools.partial(kernel, rows, cols, pieces),
        out_shape=jax.ShapeDtypeStruct((size, CB * size), jnp.bfloat16),
        in_specs=[scalars, scalars, anywhere, anywhere],
        out_specs=pl.BlockSpec(memory_space=pltpu.VMEM),
        scratch_shapes=scratch,
        compiler_params=pltpu.CompilerParams(
            collective_id=0, has_side_effects=True, vmem_limit_bytes=62 * 1024 * 1024
        ),
        name="gather_multiply_scatter",
    )(a_codes, b_codes, a_blocks, b_blocks)


def solution(mesh):
    placed = (
        P(("row", "col", "layer"), None, None),
        P(("row", "col", "layer")),
        P(("row", "col", "layer"), None, None),
        P(("row", "col", "layer")),
    )
    return jax.shard_map(
        shards, mesh=mesh, in_specs=placed, out_specs=P(("row", "layer"), "col"), check_vma=False
    )
```

```python
import functools

import jax
import jax.numpy as jnp
from jax import lax
from jax.experimental import pallas as pl
from jax.experimental.pallas import tpu as pltpu
from jax.sharding import PartitionSpec as P

RB = 4
CB = 4
KB = 6
LANES = 128
MESH = pl.DeviceIdType.MESH


def kernel(
    rows, cols, pieces,
    a_codes, b_codes, a_in, b_in, out,
    a_all, a_tags, b_tags, table, table_s, left, right, total, passing, arrived,
    a_send, a_recv, at_send, at_recv, b_send, b_recv, p_send, p_recv,
    bt_send, bt_recv, pt_send, pt_recv, here, table_sem, x_send, x_recv,
    *b_all,
):
    chips = rows // 2
    row = lax.axis_index("row")
    col = lax.axis_index("col")
    layer = lax.axis_index("layer")
    chip, core = lax.div(row, 2), lax.rem(row, 2)
    partner = {"row": chip * 2 + 1 - core}
    empty = rows * pieces

    def row_at(step):
        return lax.rem(chip + step + chips, chips) * 2 + core

    def col_at(step):
        return lax.rem(col + step + cols, cols)

    def twin_at(step):
        return lax.rem(chip + step + chips, chips) * 2 + 1 - core

    layers = 4
    after = lax.rem(layer + 1, layers)
    before = lax.rem(layer + 3, layers)
    across = lax.rem(layer + 2, layers)

    def send(src, dst, send_sem, recv_sem, where):
        copy = pltpu.make_async_remote_copy(
            src_ref=src, dst_ref=dst, send_sem=send_sem, recv_sem=recv_sem,
            device_id=where, device_id_type=MESH,
        )
        copy.start()
        sent.append(copy)

    def wait_recv(dst, send_sem, recv_sem, where):
        pltpu.make_async_remote_copy(
            src_ref=dst, dst_ref=dst, send_sem=send_sem, recv_sem=recv_sem,
            device_id=where, device_id_type=MESH,
        ).wait_recv()

    sent = []

    lane = lax.broadcasted_iota(jnp.int32, (8, LANES), 1)
    codes = jnp.full((8, LANES), -1, jnp.int32)
    for slot in range(cols):
        codes = jnp.where(lane == slot, a_codes[slot], codes)
    a_tags[col] = codes
    slot_of = lax.broadcasted_iota(jnp.int32, (rows, LANES), 0)
    codes = jnp.full((rows, LANES), -1, jnp.int32)
    for slot in range(rows):
        codes = jnp.where(slot_of == slot, b_codes[slot], codes)
    b_tags[row] = codes
    for stack in b_all:
        stack[empty] = jnp.zeros(stack.shape[1:], stack.dtype)

    local = [pltpu.make_async_copy(a_in, a_all.at[col], here.at[cols])]
    for kind in range(cols):
        local.append(
            pltpu.make_async_copy(
                b_in.at[:, kind], b_all[kind].at[pl.ds(row * pieces, pieces)], here.at[kind]
            )
        )
    for copy in local:
        copy.start()

    barrier = pltpu.get_barrier_semaphore()
    greeted = [
        {"row": row_at(1)}, {"row": row_at(-1)}, partner,
        {"col": col_at(1)}, {"col": col_at(-1)},
        {"layer": after}, {"layer": before},
    ]
    for device in greeted:
        pl.semaphore_signal(barrier, inc=1, device_id=device, device_id_type=MESH)
    pl.semaphore_wait(barrier, len(greeted))

    half_a = cols // 2
    order = [kind for pair in zip(range(half_a), range(half_a, cols)) for kind in pair]

    def ways(kind):
        return 1 if kind < half_a else -1

    def b_place(kind, source):
        return b_all[kind].at[pl.ds(source * pieces, pieces)]

    def b_forward(kind, hop, src):
        source = row_at(-ways(kind) * hop)
        send(
            src, b_place(kind, source), b_send.at[kind, hop], b_recv.at[kind, hop],
            {"row": row_at(ways(kind))},
        )

    def b_share(kind, hop, src):
        source = row_at(-ways(kind) * hop)
        send(src, b_place(kind, source), p_send.at[kind, hop], p_recv.at[kind, hop], partner)

    def b_arrive(kind, hop):
        place = b_place(kind, row_at(-ways(kind) * hop))
        wait_recv(
            place, b_send.at[kind, hop - 1], b_recv.at[kind, hop - 1], {"row": row_at(ways(kind))}
        )
        return place

    def b_shared(kind, hop):
        wait_recv(
            b_place(kind, twin_at(-ways(kind) * hop)),
            p_send.at[kind, hop], p_recv.at[kind, hop], partner,
        )

    def a_place(way, source):
        return a_all.at[source, pl.ds(half_a * way, half_a)]

    def a_forward(way, hop, src):
        step = 1 - 2 * way
        source = col_at(-step * hop)
        send(
            src, a_place(way, source), a_send.at[way, hop], a_recv.at[way, hop],
            {"col": col_at(step)},
        )

    def a_arrive(way, hop):
        step = 1 - 2 * way
        place = a_place(way, col_at(-step * hop))
        wait_recv(place, a_send.at[way, hop - 1], a_recv.at[way, hop - 1], {"col": col_at(step)})
        return place

    def tag_reach(size, way):
        return size // 2 if way == 0 else size - 1 - size // 2

    def at_forward(way, hop):
        step = 1 - 2 * way
        place = a_tags.at[col_at(-step * hop)]
        send(place, place, at_send.at[way, hop], at_recv.at[way, hop], {"col": col_at(step)})

    def bt_forward(way, hop):
        step = 1 - 2 * way
        place = b_tags.at[row_at(-step * hop)]
        send(place, place, bt_send.at[way, hop], bt_recv.at[way, hop], {"row": row_at(step)})

    def bt_share(way, hop):
        place = b_tags.at[row_at(-(1 - 2 * way) * hop)]
        send(place, place, pt_send.at[way, hop], pt_recv.at[way, hop], partner)

    for index, kind in enumerate(order):
        b_forward(kind, 0, b_in.at[:, kind])
        if index == 1:
            for way in range(2):
                if tag_reach(cols, way) > 0:
                    at_forward(way, 0)
                if tag_reach(chips, way) > 0:
                    bt_forward(way, 0)
            bt_share(0, 0)
            for way in range(2):
                a_forward(way, 0, a_in.at[pl.ds(half_a * way, half_a)])
    for kind in order:
        b_share(kind, 0, b_in.at[:, kind])

    def tags_step(hop):
        for way in range(2):
            step = 1 - 2 * way
            if hop <= tag_reach(cols, way):
                wait_recv(
                    a_tags.at[col_at(-step * hop)], at_send.at[way, hop - 1],
                    at_recv.at[way, hop - 1], {"col": col_at(step)},
                )
                if hop < tag_reach(cols, way):
                    at_forward(way, hop)
            if hop <= tag_reach(chips, way):
                wait_recv(
                    b_tags.at[row_at(-step * hop)], bt_send.at[way, hop - 1],
                    bt_recv.at[way, hop - 1], {"row": row_at(step)},
                )
                if hop < tag_reach(chips, way):
                    bt_forward(way, hop)
                bt_share(way, hop)

    def make_table():
        for way in range(2):
            for hop in range(0 if way == 0 else 1, tag_reach(chips, way) + 1):
                wait_recv(
                    b_tags.at[twin_at(-(1 - 2 * way) * hop)],
                    pt_send.at[way, hop], pt_recv.at[way, hop], partner,
                )
        owner = lax.broadcasted_iota(jnp.int32, (8, LANES), 0)
        tags = jnp.full((8, LANES), -1, jnp.int32)
        for source in range(cols):
            tags = jnp.where(owner == source, a_tags[source], tags)
        one = jnp.ones((8, LANES), jnp.int32)
        zero = jnp.zeros((8, LANES), jnp.int32)
        row_of = zero
        for bound in range(1, RB):
            row_of = row_of + jnp.where(tags >= bound * pieces * KB, one, zero)
        rest = tags - row_of * (pieces * KB)
        part_of = zero
        for bound in range(1, pieces):
            part_of = part_of + jnp.where(rest >= bound * KB, one, zero)
        inner_of = rest - part_of * KB
        piece = lax.rem(lane + row, cols) + cols * part_of
        live = tags >= 0
        first = jnp.where(live, (piece * KB + inner_of) * CB, -1000)
        wanted = [first + column for column in range(CB)]
        piece_b = lax.rem(slot_of + col, rows)

        def scan(source, found):
            tags_b = b_tags[source]
            position = jnp.where(tags_b >= 0, tags_b + piece_b * (KB * CB), -5000)
            found = list(found)
            for slot in range(rows):
                spot = jnp.broadcast_to(position[slot : slot + 1, :], (8, LANES))
                value = source * pieces + slot // cols
                for column in range(CB):
                    found[column] = jnp.where(wanted[column] == spot, value, found[column])
            return tuple(found)

        start = tuple(jnp.full((8, LANES), empty, jnp.int32) for _ in range(CB))
        found = lax.fori_loop(0, rows, scan, start)
        for column in range(CB):
            table[column] = found[column]
        table[CB] = jnp.where(live, row_of, -1)
        copy = pltpu.make_async_copy(table, table_s, table_sem)
        copy.start()
        copy.wait()

    def a_pass(hop):
        for way in range(2):
            place = a_arrive(way, hop)
            if hop < cols - 1:
                a_forward(way, hop, place)

    homes = [across, after, before, layer]

    def slot_for(kind):
        return lax.rem(kind + col + rows - row, cols)

    def place_left(kind):
        pair, at = order.index(kind) // 2, order.index(kind) % 2 * cols * LANES
        slot = slot_for(kind)
        for source in range(cols):
            block = a_all[source, slot]
            home = table_s[CB, source, slot]
            for target in range(RB):
                left[pair, pl.ds(target * LANES, LANES), pl.ds(at + source * LANES, LANES)] = (
                    jnp.where(home == homes[target], block, jnp.zeros_like(block))
                )

    def place_right(kind, index):
        local[1 + kind].wait()
        for hop in range(chips):
            b_shared(kind, hop)
        slot = slot_for(kind)
        for source in range(cols):
            for column in range(CB):
                right[pl.ds((index * cols + source) * LANES, LANES), pl.ds(column * LANES, LANES)] = (
                    b_all[kind][table_s[column, source, slot]]
                )

    wide = CB * LANES // 2

    def multiply(kinds, first_row, row_count, is_first):
        for half in range(2):
            product = jnp.dot(
                left[order.index(kinds[0]) // 2, pl.ds(first_row * LANES, row_count * LANES), :],
                right[:, pl.ds(half * wide, wide)],
                preferred_element_type=jnp.float32,
            ).reshape(row_count, LANES, wide)
            part = pl.ds(first_row, row_count)
            total[part, half] = product if is_first else total[part, half] + product

    table_after = max(tag_reach(cols, 0), tag_reach(chips, 0))
    progress = {"a": 1, "table": False, "left": 0}

    def a_until(event):
        while progress["a"] < cols and event >= 7 * progress["a"] - 5:
            a_pass(progress["a"])
            progress["a"] += 1
            if progress["a"] == cols:
                local[0].wait()

    def one_left():
        if progress["a"] == cols and progress["table"] and progress["left"] < cols:
            place_left(order[progress["left"]])
            progress["left"] += 1

    for hop in range(1, chips - 1):
        for index, kind in enumerate(order):
            place = b_arrive(kind, hop)
            b_forward(kind, hop, place)
            b_share(kind, hop, place)
            a_until((hop - 1) * cols + index)
            one_left()
        tags_step(hop)
        if hop == table_after:
            make_table()
            progress["table"] = True
    for hop in range(max(chips - 1, 1), table_after + 1):
        tags_step(hop)
    if not progress["table"]:
        make_table()
        progress["table"] = True
    a_until(7 * cols)

    pairs = [order[i : i + 2] for i in range(0, cols, 2)]
    early = pairs[: max(len(pairs) - 1, 0)]
    late = [kind for pair in pairs[len(early) :] for kind in pair]

    def finish(pair):
        for kind in pair:
            b_share(kind, chips - 1, b_arrive(kind, chips - 1))
            one_left()

    finish(pairs[0])
    for index, pair in enumerate(pairs):
        if index + 1 < len(pairs):
            finish(pairs[index + 1])
        if pair in early:
            for part, kind in enumerate(pair):
                place_right(kind, part)
            multiply(pair, 0, RB, index == 0)
    for index, kind in enumerate(late):
        place_right(kind, index)

    to_after, to_before = {"layer": after}, {"layer": before}

    def x_send_to(index, src, dst, where):
        send(src, dst, x_send.at[index], x_recv.at[index], where)

    multiply(late, 0, 1, not early)
    x_send_to(0, total.at[0, 0], passing.at[0], to_after)
    x_send_to(1, total.at[0, 1], passing.at[1], to_before)
    multiply(late, 1, 2, not early)
    x_send_to(2, total.at[1, 1], arrived.at[0, 1], to_after)
    x_send_to(3, total.at[2, 0], arrived.at[1, 0], to_before)
    multiply(late, 3, 1, not early)
    wait_recv(passing.at[0], x_send.at[0], x_recv.at[0], to_after)
    total[1, 0] = total[1, 0] + passing[0]
    x_send_to(4, total.at[1, 0], arrived.at[0, 0], to_after)
    wait_recv(passing.at[1], x_send.at[1], x_recv.at[1], to_before)
    total[2, 1] = total[2, 1] + passing[1]
    x_send_to(5, total.at[2, 1], arrived.at[1, 1], to_before)
    for copy in sent:
        copy.wait_send()
    wait_recv(arrived.at[0, 1], x_send.at[2], x_recv.at[2], to_after)
    wait_recv(arrived.at[1, 0], x_send.at[3], x_recv.at[3], to_before)
    wait_recv(arrived.at[0, 0], x_send.at[4], x_recv.at[4], to_after)
    wait_recv(arrived.at[1, 1], x_send.at[5], x_recv.at[5], to_before)
    for half in range(2):
        out[:, pl.ds(half * wide, wide)] = (
            total[3, half] + arrived[0, half] + arrived[1, half]
        ).astype(out.dtype)


def shards(a_blocks, a_codes, b_blocks, b_codes):
    rows = lax.axis_size("row")
    cols = lax.axis_size("col")
    pieces = rows // cols
    chips = rows // 2
    size = a_blocks.shape[1]
    b_blocks = b_blocks.reshape(pieces, cols, size, size)
    anywhere = pl.BlockSpec(memory_space=pl.ANY)
    scalars = pl.BlockSpec(memory_space=pltpu.SMEM)
    dma = pltpu.SemaphoreType.DMA
    wide = CB * size // 2
    scratch = [
        pltpu.VMEM((cols, cols, size, size), jnp.bfloat16),
        pltpu.VMEM((cols, 8, LANES), jnp.int32),
        pltpu.VMEM((rows, rows, LANES), jnp.int32),
        pltpu.VMEM((CB + 1, 8, LANES), jnp.int32),
        pltpu.SMEM((CB + 1, 8, LANES), jnp.int32),
        pltpu.VMEM((cols // 2, RB * size, 2 * cols * size), jnp.bfloat16),
        pltpu.VMEM((2 * cols * size, CB * size), jnp.bfloat16),
        pltpu.VMEM((RB, 2, size, wide), jnp.float32),
        pltpu.VMEM((2, size, wide), jnp.float32),
        pltpu.VMEM((2, 2, size, wide), jnp.float32),
        dma((2, cols)), dma((2, cols)), dma((2, cols)), dma((2, cols)),
        dma((cols, chips)), dma((cols, chips)), dma((cols, chips)), dma((cols, chips)),
        dma((2, chips)), dma((2, chips)), dma((2, chips)), dma((2, chips)),
        dma((cols + 1,)), dma(()), dma((6,)), dma((6,)),
    ] + [pltpu.VMEM((rows * pieces + 1, size, size), jnp.bfloat16)] * cols
    return pl.pallas_call(
        functools.partial(kernel, rows, cols, pieces),
        out_shape=jax.ShapeDtypeStruct((size, CB * size), jnp.bfloat16),
        in_specs=[scalars, scalars, anywhere, anywhere],
        out_specs=pl.BlockSpec(memory_space=pltpu.VMEM),
        scratch_shapes=scratch,
        compiler_params=pltpu.CompilerParams(
            collective_id=0, has_side_effects=True, vmem_limit_bytes=62 * 1024 * 1024
        ),
        name="gather_multiply_scatter",
    )(a_codes, b_codes, a_blocks, b_blocks)


def solution(mesh):
    placed = (
        P(("row", "col", "layer"), None, None),
        P(("row", "col", "layer")),
        P(("row", "col", "layer"), None, None),
        P(("row", "col", "layer")),
    )
    return jax.shard_map(
        shards, mesh=mesh, in_specs=placed, out_specs=P(("row", "layer"), "col"), check_vma=False
    )
```
